32 devices in a mesh: grp: 1, ex: 32 (over z, y, x, core).
Axes of the slice: x: 2, y: 2, z: 4, core: 2. Of those that a mesh axis runs over, the one named last changes fastest.
Arguments:
- example_inputs: bfloat16 [32, 1024, 4096], P(('grp', 'ex')), may hold values from -70 to 70, as said below
- output_grads: bfloat16 [32, 1024, 1024], P(('grp', 'ex')), may hold values from -70 to 70, as said below
- proj_in: bfloat16 [128, 4096], replicated, may hold values from -0.09375 to 0.09375
- proj_out: bfloat16 [64, 1024], replicated, may hold values from -0.1875 to 0.1875
- test_grads: bfloat16 [128, 8192], P('ex'), may hold values from -6 to 6
Outputs:
- scores: float32 [32, 128], P(('grp', 'ex'))
The draws below stay inside these ranges and needn't reach their ends.
Inputs may be any that keep to these rules, and one draw needn't show every extreme that they name: `example_inputs`: entries of the candidates' layer inputs lie within this range. `output_grads`: entries of the output gradients lie within this range.
All inputs are finite; a program needn't handle non-finite values.
Results may differ from the reference program's by a relative error of at most 0.0082.
Values may be sent and summed in bfloat16 or wider, within the bound.
A program may use at most 128 MiB of HBM per device.

```python
import jax
import jax.numpy as jnp
from jax import lax

D = 4096
KVW = 1024
K_IN = 128
K_OUT = 64
TOK_EX = 1024
EXAMPLES = 32
TESTS = 128
KDIM = 8192


def scaled_field(key, shared_key, width, rising):
    noise_key, row_key, col_key = jax.random.split(key, 3)
    position = jnp.arange(EXAMPLES, dtype=jnp.float32) / max(EXAMPLES - 1, 1)
    order_idx = jax.random.permutation(jax.random.fold_in(shared_key, 7), EXAMPLES)
    shuffled = position[order_idx]
    if rising:
        heavy_share = 0.8 * shuffled + 0.2 * position
    else:
        heavy_share = 0.8 * (1.0 - shuffled) + 0.2 * (1.0 - position)
    base_scale = 3.0 * jnp.power(10.0, 1.5 * heavy_share - 1.5)
    row_scale = base_scale * jnp.exp(jax.random.uniform(row_key, (EXAMPLES,), jnp.float32, -0.2, 0.2))
    col_scale = jnp.exp(jax.random.uniform(col_key, (width,), jnp.float32, jnp.log(0.3), jnp.log(3.0)))
    noise = jnp.clip(jax.random.normal(noise_key, (EXAMPLES, TOK_EX, width), jnp.float32), -6.0, 6.0)
    values = noise * row_scale[:, None, None] * col_scale[None, None, :]
    return values.astype(jnp.bfloat16)


def draw_example_inputs(key, part):
    return scaled_field(jax.random.fold_in(key, 11), key, D, True)


def draw_output_grads(key, part):
    return scaled_field(jax.random.fold_in(key, 23), key, KVW, False)


def steps_of(stream_key, dims, cuts, low, largest):
    loudness = 1.0
    for axis_at, shards_of in cuts:
        heights = jax.random.uniform(jax.random.fold_in(jax.random.fold_in(stream_key, 6), axis_at), (shards_of,), jnp.float32, low / len(cuts), largest / len(cuts))
        loudness = loudness * jnp.repeat(jnp.exp(heights), dims[axis_at] // shards_of).reshape((-1,) + (1,) * (len(dims) - 1 - axis_at))
    return loudness


def bell_draw(key, dims, deviation, most, pieces=(), kind=jnp.bfloat16):
    result = jax.random.normal(key, dims, jnp.float32) * deviation
    if len(pieces) > 0:
        result = steps_of(key, dims, pieces, -0.22, 0.18) * result
    return jnp.clip(result, min=-most, max=most).astype(kind)


def setup_inputs(seed: int = 0, part: int = 0) -> dict:
    key_list = jax.random.split(jax.random.key(seed), 6)
    part_keys = jax.random.split(jax.random.fold_in(key_list[5], part), 6)
    example_inputs = draw_example_inputs(jax.random.fold_in(jax.random.fold_in(key_list[5], part), 71), part)
    output_grads = draw_output_grads(jax.random.fold_in(jax.random.fold_in(key_list[5], part), 71), part)
    proj_in = bell_draw(key_list[2], (K_IN, D), D ** -0.5, 0.09375)
    proj_out = bell_draw(key_list[3], (K_OUT, KVW), KVW ** -0.5, 0.1875)
    test_grads = bell_draw(key_list[4], (TESTS, KDIM), 1.0, 6.0, ((0, 32),))
    return {"example_inputs": example_inputs, "output_grads": output_grads, "proj_in": proj_in, "proj_out": proj_out, "test_grads": test_grads}


def damped_inverse(cov, width):
    identity = jnp.eye(width, dtype=jnp.float32)
    damped = cov + 0.1 * jnp.trace(cov) / width * identity
    factor = jnp.linalg.cholesky(damped)
    lower_inv = lax.linalg.triangular_solve(factor, identity, left_side=True, lower=True)
    return jnp.dot(lower_inv.T, lower_inv, precision=lax.Precision.HIGHEST)

def reference(example_inputs, output_grads, proj_in, proj_out, test_grads):

    def project_one(example_pair):
        inputs_one, grads_one = example_pair
        feat = jnp.dot(inputs_one.astype(jnp.float32), proj_in.T.astype(jnp.float32), preferred_element_type=jnp.float32).astype(jnp.bfloat16)
        back = jnp.dot(grads_one.astype(jnp.float32), proj_out.T.astype(jnp.float32), preferred_element_type=jnp.float32).astype(jnp.bfloat16)
        return (feat, back)
    feat_proj, grad_proj = lax.map(project_one, (example_inputs, output_grads))
    feat32 = feat_proj.astype(jnp.float32)
    grad32 = grad_proj.astype(jnp.float32)
    grads = jnp.einsum('eto,eti->eoi', grad32, feat32, precision=lax.Precision.HIGHEST)
    total_tokens = EXAMPLES * TOK_EX
    flat_feat = feat32.reshape(-1, K_IN)
    flat_grad = grad32.reshape(-1, K_OUT)
    cov_in = jnp.dot(flat_feat.T, flat_feat, precision=lax.Precision.HIGHEST) / total_tokens
    cov_out = jnp.dot(flat_grad.T, flat_grad, precision=lax.Precision.HIGHEST) / total_tokens
    inverse_in = damped_inverse(cov_in, K_IN)
    inverse_out = damped_inverse(cov_out, K_OUT)
    left = jnp.einsum('oa,eai->eoi', inverse_out, grads, precision=lax.Precision.HIGHEST)
    both = jnp.einsum('eoa,ai->eoi', left, inverse_in, precision=lax.Precision.HIGHEST)
    precond = both.reshape(EXAMPLES, K_OUT * K_IN).astype(jnp.bfloat16)
    scale = 4.0 / (K_IN * K_OUT * TOK_EX) ** 0.5
    return jnp.dot(precond.astype(jnp.float32), test_grads.T.astype(jnp.float32), preferred_element_type=jnp.float32) * scale
```

```python
import functools
import math

import jax
import jax.numpy as jnp
from jax import lax
from jax.experimental import pallas as pl
from jax.experimental.pallas import tpu as pltpu
from jax.sharding import PartitionSpec as P

MESH = pl.DeviceIdType.MESH
HIGHEST = lax.Precision.HIGHEST
F32 = jnp.float32
BF16 = jnp.bfloat16
DAMP = 0.1
NT = (((1,), (1,)), ((), ()))
TN = (((0,), (0,)), ((), ()))


def eye(n):
    return lax.broadcasted_iota(jnp.int32, (n, n), 0) == lax.broadcasted_iota(
        jnp.int32, (n, n), 1
    )


def split(a):
    hi = a.astype(BF16)
    lo = (a - hi.astype(F32)).astype(BF16)
    return hi, lo


def wide_dot(a, b):
    n = b.shape[1]
    row = jnp.concatenate(split(b), axis=1)
    both = jnp.dot(
        jnp.concatenate(split(a), axis=1),
        jnp.concatenate([row, row], axis=0),
        preferred_element_type=F32,
    )
    return both[:, :n] + both[:, n:]


def plan(n, target=1e-3):
    low, high = DAMP / n, 1.0 + DAMP / n
    err = (high - low) / (high + low)
    factors = []
    while err > target:
        factors.append(2.0 / (2.0 - err * err))
        err = err * err / (2.0 - err * err)
    return 2.0 / (high + low), factors


def inverses(sums):
    state = []
    for s in sums:
        n = s.shape[0]
        diag = eye(n)
        trace = jnp.sum(
            jnp.sum(jnp.where(diag, s, 0.0), axis=1, keepdims=True), axis=0, keepdims=True
        )
        inv_trace = 1.0 / trace
        b = s * inv_trace + jnp.where(diag, DAMP / n, 0.0)
        first, factors = plan(n)
        x = jnp.where(diag, first, 0.0)
        y = first * b
        state.append([b, x, y, inv_trace, factors])
    for step in range(max(len(st[4]) for st in state)):
        for st in state:
            b, x, y, _, factors = st
            if step >= len(factors):
                continue
            n = b.shape[0]
            c = factors[step]
            if step == 0:
                yy = wide_dot(y, y)
                xy = x[0:1, 0:1] * y
            else:
                prod = wide_dot(jnp.concatenate([x, y], axis=0), y)
                xy, yy = prod[:n], prod[n:]
            st[1] = c * (2.0 * x - xy)
            st[2] = c * (2.0 * y - yy)
    out = []
    for b, x, _, inv_trace, _ in state:
        n = b.shape[0]
        rest = jnp.where(eye(n), 1.0, 0.0) - jnp.dot(
            b, x, precision=HIGHEST, preferred_element_type=F32
        )
        out.append((x + wide_dot(x, rest)) * inv_trace)
    return out


def kernel(
    inner, outer, chunks, tokens, scale,
    x_hbm, g_hbm, pin_hbm, pout_hbm, test_hbm, out_ref,
    x_buf, g_buf, pin_buf, pout_buf, tests, cov, moments, rs_buf, z_buf, full, grads,
    pre, flat, sbuf, rbuf,
    in_sem, t_send, t_recv, rs_send, rs_recv, g_send, g_recv, z_send, z_recv,
    ag_send, ag_recv, s_send, s_recv,
):
    k_in, k_out = pin_buf.shape[0], pout_buf.shape[0]
    me = lax.axis_index("ex")
    p, z = lax.rem(me, inner), lax.div(me, inner)
    rows = moments.shape[0] // inner
    step_rows = x_buf.shape[1]

    def at_inner(k):
        return z * inner + lax.rem(p + k, inner)

    def at_outer(k):
        return lax.rem(z + k, outer) * inner + p

    def remote(src, dst, send, recv, device):
        return pltpu.make_async_remote_copy(
            src_ref=src, dst_ref=dst, send_sem=send, recv_sem=recv,
            device_id={"ex": device}, device_id_type=MESH,
        )

    barrier = pltpu.get_barrier_semaphore()
    for k in range(1, inner):
        pl.semaphore_signal(barrier, inc=1, device_id={"ex": at_inner(k)}, device_id_type=MESH)
    for k in range(1, outer):
        pl.semaphore_signal(barrier, inc=1, device_id={"ex": at_outer(k)}, device_id_type=MESH)

    loads = [
        pltpu.make_async_copy(pout_hbm, pout_buf, in_sem.at[0]),
        pltpu.make_async_copy(g_hbm, g_buf, in_sem.at[1]),
        pltpu.make_async_copy(pin_hbm, pin_buf, in_sem.at[2]),
    ]
    own_tests = pltpu.make_async_copy(test_hbm, tests.at[z], in_sem.at[3])

    def x_load(i):
        return pltpu.make_async_copy(
            x_hbm.at[pl.ds(i * step_rows, step_rows)], x_buf.at[i], in_sem.at[4 + i]
        )

    for c in loads:
        c.start()
    own_tests.start()
    for i in range(chunks):
        x_load(i).start()

    pl.semaphore_wait(barrier, inner + outer - 2)
    test_copies = [
        remote(test_hbm, tests.at[z], t_send.at[k], t_recv.at[k], at_outer(k))
        for k in range(1, outer)
    ]
    for c in test_copies:
        c.start()

    for c in loads:
        c.wait()
    cov[...] = jnp.zeros_like(cov)

    def project(i, carry):
        begin = pl.multiple_of(i * step_rows, step_rows)
        back = lax.dot_general(
            g_buf[pl.ds(begin, step_rows), :], pout_buf[...], NT, preferred_element_type=F32
        ).astype(BF16)
        x_load(i).wait()
        feat = lax.dot_general(
            x_buf[i], pin_buf[...], NT, preferred_element_type=F32
        ).astype(BF16)
        both = jnp.concatenate([feat, back], axis=1)
        cov[...] += lax.dot_general(both, both, TN, preferred_element_type=F32)
        return carry

    lax.fori_loop(0, chunks, project, 0)

    moments[0:k_in, :] = cov[0:k_in, 0:k_in]
    moments[k_in : k_in + k_out, :] = jnp.concatenate(
        [cov[k_in : k_in + k_out, k_in : k_in + k_out], jnp.zeros((k_out, k_in - k_out), F32)],
        axis=1,
    )
    grads[p] = cov[k_in : k_in + k_out, 0:k_in]

    rs_copies = []
    for k in range(1, inner):
        peer = lax.rem(p + k, inner)
        rs_copies.append(
            remote(
                moments.at[pl.ds(pl.multiple_of(peer * rows, 8), rows)],
                rs_buf.at[p], rs_send.at[k], rs_recv.at[k], at_inner(k),
            )
        )
    for c in rs_copies:
        c.start()
    rs_buf[p] = moments[pl.ds(pl.multiple_of(p * rows, 8), rows), :]
    for c in rs_copies:
        c.wait_recv()
    part = rs_buf[0]
    for j in range(1, inner):
        part = part + rs_buf[j]
    z_buf[z] = part
    z_copies = [
        remote(z_buf.at[z], z_buf.at[z], z_send.at[k], z_recv.at[k], at_outer(k))
        for k in range(1, outer)
    ]
    for c in z_copies:
        c.start()
    g_copies = [
        remote(grads.at[p], grads.at[p], g_send.at[k], g_recv.at[k], at_inner(k))
        for k in range(1, inner)
    ]
    for c in g_copies:
        c.start()
    for c in z_copies:
        c.wait_recv()
    total = z_buf[0]
    for j in range(1, outer):
        total = total + z_buf[j]
    mine = full.at[pl.ds(pl.multiple_of(p * rows, 8), rows)]
    mine[...] = total
    ag_copies = [
        remote(mine, mine, ag_send.at[k], ag_recv.at[k], at_inner(k)) for k in range(1, inner)
    ]
    for c in ag_copies:
        c.start()
    for c in g_copies:
        c.wait_recv()
    for c in ag_copies:
        c.wait_recv()

    sum_in = full[0:k_in, :]
    sum_out = full[k_in : k_in + k_out, 0:k_out]
    inv_in, inv_out = inverses([sum_in, sum_out])
    inv_in = inv_in * tokens
    inv_out = inv_out * tokens
    right = jnp.dot(
        grads[...].reshape(inner * k_out, k_in), inv_in,
        precision=HIGHEST, preferred_element_type=F32,
    )
    for e in range(inner):
        pre[e * k_out : (e + 1) * k_out, :] = jnp.dot(
            inv_out, right[e * k_out : (e + 1) * k_out],
            precision=HIGHEST, preferred_element_type=F32,
        )
    for o in range(k_out):
        flat[:, o * k_in : (o + 1) * k_in] = pre[pl.ds(o, inner, stride=k_out), :]
    precond = flat[...].astype(BF16)

    own_tests.wait()
    for c in test_copies:
        c.wait_recv()
    per = tests.shape[1]
    width = out_ref.shape[1]
    placed = jnp.zeros((inner, width), F32)
    for j in range(outer):
        block = lax.dot_general(precond, tests[j], NT, preferred_element_type=F32)
        first = (j * inner + p) * per
        put = lax.broadcasted_iota(jnp.int32, (per, width), 1) == (
            first + lax.broadcasted_iota(jnp.int32, (per, width), 0)
        )
        placed = placed + jnp.dot(
            block, jnp.where(put, 1.0, 0.0), precision=HIGHEST, preferred_element_type=F32
        )
    for e in range(inner):
        sbuf[e] = placed[e : e + 1]
    s_copies = [
        remote(
            sbuf.at[lax.rem(p + k, inner)], rbuf.at[p], s_send.at[k], s_recv.at[k], at_inner(k)
        )
        for k in range(1, inner)
    ]
    for c in s_copies:
        c.start()
    rbuf[p] = sbuf[p]
    for c in s_copies:
        c.wait_recv()
    score = rbuf[0]
    for j in range(1, inner):
        score = score + rbuf[j]
    out_ref[...] = score * scale
    for group in (test_copies, rs_copies, z_copies, g_copies, ag_copies, s_copies):
        for c in group:
            c.wait_send()


def on_device(devices, x, g, proj_in, proj_out, tests):
    _, tok, _ = x.shape
    k_in, k_out = proj_in.shape[0], proj_out.shape[0]
    inner = math.gcd(devices, 8)
    outer = devices // inner
    per = tests.shape[0]
    chunks = 4
    total_tokens = tok * devices
    scale = 4.0 / (k_in * k_out * tok) ** 0.5
    height = k_in + k_out
    any_space = pl.BlockSpec(memory_space=pl.ANY)
    dma = pltpu.SemaphoreType.DMA
    return pl.pallas_call(
        functools.partial(kernel, inner, outer, chunks, float(total_tokens), scale),
        out_shape=jax.ShapeDtypeStruct((1, per * devices), F32),
        in_specs=[any_space] * 5,
        out_specs=pl.BlockSpec(memory_space=pltpu.VMEM),
        scratch_shapes=[
            pltpu.VMEM((chunks, tok // chunks, x.shape[2]), BF16),
            pltpu.VMEM(g.shape[1:], BF16),
            pltpu.VMEM(proj_in.shape, BF16),
            pltpu.VMEM(proj_out.shape, BF16),
            pltpu.VMEM((outer,) + tests.shape, BF16),
            pltpu.VMEM((height, height), F32),
            pltpu.VMEM((height, k_in), F32),
            pltpu.VMEM((inner, height // inner, k_in), F32),
            pltpu.VMEM((outer, height // inner, k_in), F32),
            pltpu.VMEM((height, k_in), F32),
            pltpu.VMEM((inner, k_out, k_in), F32),
            pltpu.VMEM((inner * k_out, k_in), F32),
            pltpu.VMEM((inner, k_out * k_in), F32),
            pltpu.VMEM((inner, 1, per * devices), F32),
            pltpu.VMEM((inner, 1, per * devices), F32),
            dma((4 + chunks,)),
            dma((outer,)), dma((outer,)),
            dma((inner,)), dma((inner,)),
            dma((inner,)), dma((inner,)),
            dma((outer,)), dma((outer,)),
            dma((inner,)), dma((inner,)),
            dma((inner,)), dma((inner,)),
        ],
        compiler_params=pltpu.CompilerParams(
            collective_id=0, has_side_effects=True, vmem_limit_bytes=56 * 1024 * 1024
        ),
    )(x[0], g[0], proj_in, proj_out, tests)


def solution(mesh):
    return jax.shard_map(
        functools.partial(on_device, mesh.shape["ex"]),
        mesh=mesh,
        in_specs=(
            P(("grp", "ex"), None, None),
            P(("grp", "ex"), None, None),
            P(),
            P(),
            P("ex", None),
        ),
        out_specs=P(("grp", "ex"), None),
        check_vma=False,
    )
```

```python
import functools
import math

import jax
import jax.numpy as jnp
from jax import lax
from jax.experimental import pallas as pl
from jax.experimental.pallas import tpu as pltpu
from jax.sharding import PartitionSpec as P

MESH = pl.DeviceIdType.MESH
HIGHEST = lax.Precision.HIGHEST
F32 = jnp.float32
BF16 = jnp.bfloat16
DAMP = 0.1
NT = (((1,), (1,)), ((), ()))
TN = (((0,), (0,)), ((), ()))


def eye(n):
    return lax.broadcasted_iota(jnp.int32, (n, n), 0) == lax.broadcasted_iota(
        jnp.int32, (n, n), 1
    )


def split(a):
    hi = a.astype(BF16)
    lo = (a - hi.astype(F32)).astype(BF16)
    return hi, lo


def wide_dot(a, b):
    n = b.shape[1]
    row = jnp.concatenate(split(b), axis=1)
    both = jnp.dot(
        jnp.concatenate(split(a), axis=1),
        jnp.concatenate([row, row], axis=0),
        preferred_element_type=F32,
    )
    return both[:, :n] + both[:, n:]


def plan(n, target=2e-3):
    low, high = DAMP / n, 1.0 + DAMP / n
    err = (high - low) / (high + low)
    factors = []
    while err > target:
        factors.append(2.0 / (2.0 - err * err))
        err = err * err / (2.0 - err * err)
    return 2.0 / (high + low), factors


def inverses(sums):
    state = []
    for s, n in sums:
        size = s.shape[0]
        diag = eye(size)
        trace = jnp.sum(
            jnp.sum(jnp.where(diag, s, 0.0), axis=1, keepdims=True), axis=0, keepdims=True
        )
        inv_trace = 1.0 / trace
        b = s * inv_trace + jnp.where(diag, DAMP / n, 0.0)
        first, factors = plan(n)
        if size > n:
            beyond = lax.broadcasted_iota(jnp.int32, (size, size), 0) >= n
            b = jnp.where(diag & beyond, 1.0 / first, b)
        x = jnp.where(diag, first, 0.0)
        y = first * b
        state.append([b, x, y, inv_trace, factors, first])
    for step in range(max(len(st[4]) for st in state)):
        for st in state:
            b, x, y, _, factors, plan_first = st
            if step >= len(factors):
                continue
            n = b.shape[0]
            c = factors[step]
            if step == 0:
                yy = wide_dot(y, y)
                xy = plan_first * y
            else:
                prod = wide_dot(jnp.concatenate([x, y], axis=0), y)
                xy, yy = prod[:n], prod[n:]
            st[1] = c * (2.0 * x - xy)
            st[2] = c * (2.0 * y - yy)
    out = []
    for b, x, _, inv_trace, _, _ in state:
        n = b.shape[0]
        rest = jnp.where(eye(n), 1.0, 0.0) - jnp.dot(
            b, x, precision=HIGHEST, preferred_element_type=F32
        )
        out.append((x + wide_dot(x, rest)) * inv_trace)
    return out


def kernel(
    inner, outer, chunks, tokens,
    x_hbm, g_hbm, pin_hbm, pout_hbm, test_hbm, out_ref,
    x_buf, g_buf, pin_buf, pout_buf, tests, cov, moments, rs_buf, z_buf, full, grads,
    pre, flat, sbuf, rbuf, acc,
    in_sem, t_send, t_recv, rs_send, rs_recv, g_send, g_recv, z_send, z_recv,
    ag_send, ag_recv, s_send, s_recv,
):
    k_in, k_out = pin_buf.shape[0], pout_buf.shape[0]
    me = lax.axis_index("ex")
    p, z = lax.rem(me, inner), lax.div(me, inner)
    rows = moments.shape[0] // inner
    step_cols = x_buf.shape[2]

    def at_inner(k):
        return z * inner + lax.rem(p + k, inner)

    def at_outer(k):
        return lax.rem(z + k, outer) * inner + p

    def remote(src, dst, send, recv, device):
        return pltpu.make_async_remote_copy(
            src_ref=src, dst_ref=dst, send_sem=send, recv_sem=recv,
            device_id={"ex": device}, device_id_type=MESH,
        )

    barrier = pltpu.get_barrier_semaphore()
    for k in range(1, inner):
        pl.semaphore_signal(barrier, inc=1, device_id={"ex": at_inner(k)}, device_id_type=MESH)
    for k in range(1, outer):
        pl.semaphore_signal(barrier, inc=1, device_id={"ex": at_outer(k)}, device_id_type=MESH)

    loads = [
        pltpu.make_async_copy(pout_hbm, pout_buf, in_sem.at[0]),
        pltpu.make_async_copy(pin_hbm, pin_buf, in_sem.at[1]),
    ]
    own_tests = pltpu.make_async_copy(test_hbm, tests.at[z], in_sem.at[2])

    def x_load(i):
        return pltpu.make_async_copy(
            x_hbm.at[:, i * step_cols : (i + 1) * step_cols], x_buf.at[i], in_sem.at[5 + i]
        )

    mid = g_buf.shape[0] // 2
    quarter = mid // 2
    g_loads = [
        pltpu.make_async_copy(
            g_hbm.at[pl.ds(h * mid, mid)], g_buf.at[pl.ds(h * mid, mid)], in_sem.at[3 + h]
        )
        for h in range(2)
    ]
    loads[0].start()
    for c in g_loads:
        c.start()
    loads[1].start()
    own_tests.start()
    for i in range(chunks):
        x_load(i).start()

    test_copies = [
        remote(test_hbm, tests.at[z], t_send.at[k], t_recv.at[k], at_outer(k))
        for k in range(1, outer)
    ]
    loads[0].wait()
    halves = (slice(0, mid), slice(mid, 2 * mid))
    backs = []
    for h in range(2):
        g_loads[h].wait()
        backs += [
            lax.dot_general(
                g_buf[q : q + quarter, :], pout_buf[...], NT, preferred_element_type=F32
            ).astype(BF16)
            for q in (h * mid, h * mid + quarter)
        ]
    loads[1].wait()
    for i in range(chunks):
        x_load(i).wait()
        if i == 1:
            pl.semaphore_wait(barrier, inner + outer - 2)
            for c in test_copies:
                c.start()
        weights = pin_buf[:, i * step_cols : (i + 1) * step_cols]
        feats = [
            lax.dot_general(x_buf[i, h, :], weights, NT, preferred_element_type=F32)
            for h in halves
        ]
        for h, feat in zip(halves, feats):
            if i == 0:
                acc[h, :] = feat
            else:
                acc[h, :] += feat
    parts = []
    for h in range(2):
        back = jnp.concatenate(backs[2 * h : 2 * h + 2], axis=0)
        both = jnp.concatenate([acc[halves[h], :].astype(BF16), back], axis=1)
        parts.append(lax.dot_general(both, both, TN, preferred_element_type=F32))
    cov[...] = parts[0] + parts[1]

    half = k_in // 2
    moments[0:half, :] = cov[0:half, 0:k_in]
    moments[half:k_in, half:k_in] = cov[half:k_in, half:k_in]
    moments[half:k_in, 0:half] = cov[k_in : k_in + k_out, k_in : k_in + k_out]
    grads[p] = cov[k_in : k_in + k_out, 0:k_in]

    rs_copies = []
    for k in range(1, inner):
        peer = lax.rem(p + k, inner)
        rs_copies.append(
            remote(
                moments.at[pl.ds(pl.multiple_of(peer * rows, 8), rows)],
                rs_buf.at[p], rs_send.at[k], rs_recv.at[k], at_inner(k),
            )
        )
    for c in rs_copies:
        c.start()
    rs_buf[p] = moments[pl.ds(pl.multiple_of(p * rows, 8), rows), :]
    for c in rs_copies:
        c.wait_recv()
    part = rs_buf[0]
    for j in range(1, inner):
        part = part + rs_buf[j]
    z_buf[z] = part
    z_copies = [
        remote(z_buf.at[z], z_buf.at[z], z_send.at[k], z_recv.at[k], at_outer(k))
        for k in range(1, outer)
    ]
    for c in z_copies:
        c.start()
    g_copies = [
        remote(grads.at[p], grads.at[p], g_send.at[k], g_recv.at[k], at_inner(k))
        for k in range(1, inner)
    ]
    for c in z_copies:
        c.wait_recv()
    total = z_buf[0]
    for j in range(1, outer):
        total = total + z_buf[j]
    mine = full.at[pl.ds(pl.multiple_of(p * rows, 8), rows)]
    mine[...] = total
    ag_copies = [
        remote(mine, mine, ag_send.at[k], ag_recv.at[k], at_inner(k)) for k in range(1, inner)
    ]
    for c in ag_copies:
        c.start()
    for c in g_copies:
        c.start()
    for c in ag_copies:
        c.wait_recv()

    top, low = full[0:half, :], full[half:k_in, :]
    corner = jnp.concatenate([top.T[half:k_in, :], low[:, half:]], axis=1)
    sum_in = jnp.concatenate([top, corner], axis=0)
    sum_out = jnp.concatenate([low[:, 0:half], jnp.zeros((half, half), F32)], axis=1)
    sum_out = jnp.concatenate([sum_out, jnp.zeros((half, k_in), F32)], axis=0)
    inv_in, inv_out = inverses([(sum_in, k_in), (sum_out, k_out)])
    inv_in = inv_in * tokens
    inv_out = inv_out[0:k_out, 0:k_out] * tokens
    for c in g_copies:
        c.wait_recv()
    batch = max(inner // 2, 1)
    rights = [
        jnp.dot(
            grads[e : e + batch].reshape(batch * k_out, k_in), inv_in,
            precision=HIGHEST, preferred_element_type=F32,
        )
        for e in range(0, inner, batch)
    ]
    for e in range(batch):
        for r, right in enumerate(rights):
            at = (r * batch + e) * k_out
            pre[at : at + k_out, :] = jnp.dot(
                inv_out, right[e * k_out : (e + 1) * k_out],
                precision=HIGHEST, preferred_element_type=F32,
            )
    for o in range(k_out):
        flat[:, o * k_in : (o + 1) * k_in] = pre[pl.ds(o, inner, stride=k_out), :]
    precond = flat[...].astype(BF16)

    own_tests.wait()
    for c in test_copies:
        c.wait_recv()
    per = tests.shape[1]
    width = out_ref.shape[1]
    block = lax.dot_general(
        precond, jnp.concatenate([tests[j] for j in range(outer)], axis=0), NT,
        preferred_element_type=F32,
    )
    held = lax.broadcasted_iota(jnp.int32, (outer * per, width), 0)
    place = (lax.div(held, per) * inner + p) * per + lax.rem(held, per)
    put = lax.broadcasted_iota(jnp.int32, (outer * per, width), 1) == place
    placed = jnp.dot(
        block, jnp.where(put, 1.0, 0.0), precision=HIGHEST, preferred_element_type=F32
    )
    for e in range(inner):
        sbuf[e] = placed[e : e + 1]
    s_copies = [
        remote(
            sbuf.at[lax.rem(p + k, inner)], rbuf.at[p], s_send.at[k], s_recv.at[k], at_inner(k)
        )
        for k in range(1, inner)
    ]
    for c in s_copies:
        c.start()
    rbuf[p] = sbuf[p]
    for c in s_copies:
        c.wait_recv()
    score = rbuf[0]
    for j in range(1, inner):
        score = score + rbuf[j]
    out_ref[...] = score
    for group in (test_copies, rs_copies, z_copies, g_copies, ag_copies, s_copies):
        for c in group:
            c.wait_send()


def on_device(devices, x, g, proj_in, proj_out, tests):
    _, tok, _ = x.shape
    k_in, k_out = proj_in.shape[0], proj_out.shape[0]
    inner = math.gcd(devices, 8)
    outer = devices // inner
    per = tests.shape[0]
    chunks = 4
    total_tokens = tok * devices
    scale = 4.0 / (k_in * k_out * tok) ** 0.5
    height = k_in + k_out
    any_space = pl.BlockSpec(memory_space=pl.ANY)
    dma = pltpu.SemaphoreType.DMA
    out = pl.pallas_call(
        functools.partial(kernel, inner, outer, chunks, float(total_tokens)),
        out_shape=jax.ShapeDtypeStruct((1, per * devices), F32),
        in_specs=[any_space] * 5,
        out_specs=pl.BlockSpec(memory_space=pltpu.VMEM),
        scratch_shapes=[
            pltpu.VMEM((chunks, tok, x.shape[2] // chunks), BF16),
            pltpu.VMEM(g.shape[1:], BF16),
            pltpu.VMEM(proj_in.shape, BF16),
            pltpu.VMEM(proj_out.shape, BF16),
            pltpu.VMEM((outer,) + tests.shape, BF16),
            pltpu.VMEM((height, height), F32),
            pltpu.VMEM((k_in, k_in), F32),
            pltpu.VMEM((inner, k_in // inner, k_in), F32),
            pltpu.VMEM((outer, k_in // inner, k_in), F32),
            pltpu.VMEM((k_in, k_in), F32),
            pltpu.VMEM((inner, k_out, k_in), F32),
            pltpu.VMEM((inner * k_out, k_in), F32),
            pltpu.VMEM((inner, k_out * k_in), F32),
            pltpu.VMEM((inner, 1, per * devices), F32),
            pltpu.VMEM((inner, 1, per * devices), F32),
            pltpu.VMEM((tok, k_in), F32),
            dma((5 + chunks,)),
            dma((outer,)), dma((outer,)),
            dma((inner,)), dma((inner,)),
            dma((inner,)), dma((inner,)),
            dma((outer,)), dma((outer,)),
            dma((inner,)), dma((inner,)),
            dma((inner,)), dma((inner,)),
        ],
        compiler_params=pltpu.CompilerParams(
            collective_id=0, has_side_effects=True, vmem_limit_bytes=56 * 1024 * 1024
        ),
    )(x[0], g[0], proj_in, proj_out, tests)
    return out * scale


def solution(mesh):
    return jax.shard_map(
        functools.partial(on_device, mesh.shape["ex"]),
        mesh=mesh,
        in_specs=(
            P(("grp", "ex"), None, None),
            P(("grp", "ex"), None, None),
            P(),
            P(),
            P("ex", None),
        ),
        out_specs=P(("grp", "ex"), None),
        check_vma=False,
    )
```

```python
import functools
import math

import jax
import jax.numpy as jnp
from jax import lax
from jax.experimental import pallas as pl
from jax.experimental.pallas import tpu as pltpu
from jax.sharding import PartitionSpec as P

MESH = pl.DeviceIdType.MESH
HIGHEST = lax.Precision.HIGHEST
F32 = jnp.float32
BF16 = jnp.bfloat16
DAMP = 0.1
NT = (((1,), (1,)), ((), ()))
TN = (((0,), (0,)), ((), ()))


def eye(n):
    return lax.broadcasted_iota(jnp.int32, (n, n), 0) == lax.broadcasted_iota(
        jnp.int32, (n, n), 1
    )


def split(a):
    hi = a.astype(BF16)
    lo = (a - hi.astype(F32)).astype(BF16)
    return hi, lo


def wide_dot(a, b):
    n = b.shape[1]
    row = jnp.concatenate(split(b), axis=1)
    both = jnp.dot(
        jnp.concatenate(split(a), axis=1),
        jnp.concatenate([row, row], axis=0),
        preferred_element_type=F32,
    )
    return both[:, :n] + both[:, n:]


def plan(n, target=2e-3):
    low, high = DAMP / n, 1.0 + DAMP / n
    err = (high - low) / (high + low)
    factors = []
    while err > target:
        factors.append(2.0 / (2.0 - err * err))
        err = err * err / (2.0 - err * err)
    return 2.0 / (high + low), factors


def inverses(sums):
    state = []
    for s, n in sums:
        size = s.shape[0]
        diag = eye(size)
        trace = jnp.sum(
            jnp.sum(jnp.where(diag, s, 0.0), axis=1, keepdims=True), axis=0, keepdims=True
        )
        inv_trace = 1.0 / trace
        b = s * inv_trace + jnp.where(diag, DAMP / n, 0.0)
        first, factors = plan(n)
        if size > n:
            beyond = lax.broadcasted_iota(jnp.int32, (size, size), 0) >= n
            b = jnp.where(diag & beyond, 1.0 / first, b)
        x = jnp.where(diag, first, 0.0)
        y = first * b
        state.append([b, x, y, inv_trace, factors, first])
    for step in range(max(len(st[4]) for st in state)):
        for st in state:
            b, x, y, _, factors, plan_first = st
            if step >= len(factors):
                continue
            n = b.shape[0]
            c = factors[step]
            if step == 0:
                yy = wide_dot(y, y)
                xy = plan_first * y
            else:
                prod = wide_dot(jnp.concatenate([x, y], axis=0), y)
                xy, yy = prod[:n], prod[n:]
            st[1] = c * (2.0 * x - xy)
            st[2] = c * (2.0 * y - yy)
    out = []
    for b, x, _, inv_trace, _, _ in state:
        n = b.shape[0]
        rest = jnp.where(eye(n), 1.0, 0.0) - jnp.dot(
            b, x, precision=HIGHEST, preferred_element_type=F32
        )
        out.append((x + wide_dot(x, rest)) * inv_trace)
    return out


def kernel(
    inner, outer, chunks, tokens,
    x_hbm, g_hbm, pin_hbm, pout_hbm, test_hbm, out_ref,
    x_buf, g_buf, pin_buf, pout_buf, tests, cov, moments, rs_buf, z_buf, full, grads,
    pre, flat, sbuf, rbuf, acc,
    in_sem, t_send, t_recv, rs_send, rs_recv, g_send, g_recv, z_send, z_recv,
    ag_send, ag_recv, s_send, s_recv,
):
    k_in, k_out = pin_buf.shape[0], pout_buf.shape[0]
    me = lax.axis_index("ex")
    p, z = lax.rem(me, inner), lax.div(me, inner)
    rows = moments.shape[0] // inner
    step_cols = x_buf.shape[2]

    def at_inner(k):
        return z * inner + lax.rem(p + k, inner)

    def at_outer(k):
        return lax.rem(z + k, outer) * inner + p

    def remote(src, dst, send, recv, device):
        return pltpu.make_async_remote_copy(
            src_ref=src, dst_ref=dst, send_sem=send, recv_sem=recv,
            device_id={"ex": device}, device_id_type=MESH,
        )

    barrier = pltpu.get_barrier_semaphore()
    for k in range(1, inner):
        pl.semaphore_signal(barrier, inc=1, device_id={"ex": at_inner(k)}, device_id_type=MESH)
    for k in range(1, outer):
        pl.semaphore_signal(barrier, inc=1, device_id={"ex": at_outer(k)}, device_id_type=MESH)

    pout_load = pltpu.make_async_copy(pout_hbm, pout_buf, in_sem.at[0])
    own_tests = pltpu.make_async_copy(test_hbm, tests.at[z], in_sem.at[1])

    def pin_load(i):
        cols = slice(i * step_cols, (i + 1) * step_cols)
        return pltpu.make_async_copy(
            pin_hbm.at[:, cols], pin_buf.at[:, cols], in_sem.at[4 + chunks + i]
        )

    def x_load(i):
        return pltpu.make_async_copy(
            x_hbm.at[:, i * step_cols : (i + 1) * step_cols], x_buf.at[i], in_sem.at[4 + i]
        )

    mid = g_buf.shape[0] // 2
    quarter = mid // 2
    g_loads = [
        pltpu.make_async_copy(
            g_hbm.at[pl.ds(h * mid, mid)], g_buf.at[pl.ds(h * mid, mid)], in_sem.at[2 + h]
        )
        for h in range(2)
    ]
    pout_load.start()
    for c in g_loads:
        c.start()
    for i in range(chunks):
        pin_load(i).start()
        x_load(i).start()
    own_tests.start()

    test_copies = [
        remote(test_hbm, tests.at[z], t_send.at[k], t_recv.at[k], at_outer(k))
        for k in range(1, outer)
    ]
    pout_load.wait()
    halves = (slice(0, mid), slice(mid, 2 * mid))
    backs = []
    for h in range(2):
        g_loads[h].wait()
        backs += [
            lax.dot_general(
                g_buf[q : q + quarter, :], pout_buf[...], NT, preferred_element_type=F32
            ).astype(BF16)
            for q in (h * mid, h * mid + quarter)
        ]
    pl.semaphore_wait(barrier, inner + outer - 2)
    for c in test_copies:
        c.start()
    for i in range(chunks):
        pin_load(i).wait()
        x_load(i).wait()
        weights = pin_buf[:, i * step_cols : (i + 1) * step_cols]
        feats = [
            lax.dot_general(x_buf[i, h, :], weights, NT, preferred_element_type=F32)
            for h in halves
        ]
        for h, feat in zip(halves, feats):
            if i == 0:
                acc[h, :] = feat
            else:
                acc[h, :] += feat
    parts = []
    for h in range(2):
        back = jnp.concatenate(backs[2 * h : 2 * h + 2], axis=0)
        both = jnp.concatenate([acc[halves[h], :].astype(BF16), back], axis=1)
        parts.append(lax.dot_general(both, both, TN, preferred_element_type=F32))
    cov[...] = parts[0] + parts[1]

    half = k_in // 2
    moments[0:half, :] = cov[0:half, 0:k_in]
    moments[half:k_in, half:k_in] = cov[half:k_in, half:k_in]
    moments[half:k_in, 0:half] = cov[k_in : k_in + k_out, k_in : k_in + k_out]
    grads[p] = cov[k_in : k_in + k_out, 0:k_in]

    rs_copies = []
    for k in range(1, inner):
        peer = lax.rem(p + k, inner)
        rs_copies.append(
            remote(
                moments.at[pl.ds(pl.multiple_of(peer * rows, 8), rows)],
                rs_buf.at[p], rs_send.at[k], rs_recv.at[k], at_inner(k),
            )
        )
    for c in rs_copies:
        c.start()
    rs_buf[p] = moments[pl.ds(pl.multiple_of(p * rows, 8), rows), :]
    for c in rs_copies:
        c.wait_recv()
    part = rs_buf[0]
    for j in range(1, inner):
        part = part + rs_buf[j]
    z_buf[z] = part
    z_copies = [
        remote(z_buf.at[z], z_buf.at[z], z_send.at[k], z_recv.at[k], at_outer(k))
        for k in range(1, outer)
    ]
    for c in z_copies:
        c.start()
    g_copies = [
        remote(grads.at[p], grads.at[p], g_send.at[k], g_recv.at[k], at_inner(k))
        for k in range(1, inner)
    ]
    for c in g_copies:
        c.start()
    for c in z_copies:
        c.wait_recv()
    total = z_buf[0]
    for j in range(1, outer):
        total = total + z_buf[j]
    mine = full.at[pl.ds(pl.multiple_of(p * rows, 8), rows)]
    mine[...] = total
    ag_copies = [
        remote(mine, mine, ag_send.at[k], ag_recv.at[k], at_inner(k)) for k in range(1, inner)
    ]
    for c in ag_copies:
        c.start()
    for c in ag_copies:
        c.wait_recv()

    top, low = full[0:half, :], full[half:k_in, :]
    corner = jnp.concatenate([top.T[half:k_in, :], low[:, half:]], axis=1)
    sum_in = jnp.concatenate([top, corner], axis=0)
    sum_out = jnp.concatenate([low[:, 0:half], jnp.zeros((half, half), F32)], axis=1)
    sum_out = jnp.concatenate([sum_out, jnp.zeros((half, k_in), F32)], axis=0)
    inv_in, inv_out = inverses([(sum_in, k_in), (sum_out, k_out)])
    inv_in = inv_in * tokens
    inv_out = inv_out[0:k_out, 0:k_out] * tokens
    for c in g_copies:
        c.wait_recv()
    batch = max(inner // 2, 1)
    rights = [
        jnp.dot(
            grads[e : e + batch].reshape(batch * k_out, k_in), inv_in,
            precision=HIGHEST, preferred_element_type=F32,
        )
        for e in range(0, inner, batch)
    ]
    for e in range(batch):
        for r, right in enumerate(rights):
            at = (r * batch + e) * k_out
            pre[at : at + k_out, :] = jnp.dot(
                inv_out, right[e * k_out : (e + 1) * k_out],
                precision=HIGHEST, preferred_element_type=F32,
            )
    for o in range(k_out):
        flat[:, o * k_in : (o + 1) * k_in] = pre[pl.ds(o, inner, stride=k_out), :]
    precond = flat[...].astype(BF16)

    own_tests.wait()
    for c in test_copies:
        c.wait_recv()
    per = tests.shape[1]
    width = out_ref.shape[1]
    block = lax.dot_general(
        precond, jnp.concatenate([tests[j] for j in range(outer)], axis=0), NT,
        preferred_element_type=F32,
    )
    held = lax.broadcasted_iota(jnp.int32, (outer * per, width), 0)
    place = (lax.div(held, per) * inner + p) * per + lax.rem(held, per)
    put = lax.broadcasted_iota(jnp.int32, (outer * per, width), 1) == place
    placed = jnp.dot(
        block, jnp.where(put, 1.0, 0.0), precision=HIGHEST, preferred_element_type=F32
    )
    for e in range(inner):
        sbuf[e] = placed[e : e + 1]
    s_copies = [
        remote(
            sbuf.at[lax.rem(p + k, inner)], rbuf.at[p], s_send.at[k], s_recv.at[k], at_inner(k)
        )
        for k in range(1, inner)
    ]
    for c in s_copies:
        c.start()
    rbuf[p] = sbuf[p]
    for c in s_copies:
        c.wait_recv()
    score = rbuf[0]
    for j in range(1, inner):
        score = score + rbuf[j]
    out_ref[...] = score
    for group in (test_copies, rs_copies, z_copies, g_copies, ag_copies, s_copies):
        for c in group:
            c.wait_send()


def on_device(devices, x, g, proj_in, proj_out, tests):
    _, tok, _ = x.shape
    k_in, k_out = proj_in.shape[0], proj_out.shape[0]
    inner = math.gcd(devices, 8)
    outer = devices // inner
    per = tests.shape[0]
    chunks = 8
    total_tokens = tok * devices
    scale = 4.0 / (k_in * k_out * tok) ** 0.5
    height = k_in + k_out
    any_space = pl.BlockSpec(memory_space=pl.ANY)
    dma = pltpu.SemaphoreType.DMA
    out = pl.pallas_call(
        functools.partial(kernel, inner, outer, chunks, float(total_tokens)),
        out_shape=jax.ShapeDtypeStruct((1, per * devices), F32),
        in_specs=[any_space] * 5,
        out_specs=pl.BlockSpec(memory_space=pltpu.VMEM),
        scratch_shapes=[
            pltpu.VMEM((chunks, tok, x.shape[2] // chunks), BF16),
            pltpu.VMEM(g.shape[1:], BF16),
            pltpu.VMEM(proj_in.shape, BF16),
            pltpu.VMEM(proj_out.shape, BF16),
            pltpu.VMEM((outer,) + tests.shape, BF16),
            pltpu.VMEM((height, height), F32),
            pltpu.VMEM((k_in, k_in), F32),
            pltpu.VMEM((inner, k_in // inner, k_in), F32),
            pltpu.VMEM((outer, k_in // inner, k_in), F32),
            pltpu.VMEM((k_in, k_in), F32),
            pltpu.VMEM((inner, k_out, k_in), F32),
            pltpu.VMEM((inner * k_out, k_in), F32),
            pltpu.VMEM((inner, k_out * k_in), F32),
            pltpu.VMEM((inner, 1, per * devices), F32),
            pltpu.VMEM((inner, 1, per * devices), F32),
            pltpu.VMEM((tok, k_in), F32),
            dma((4 + 2 * chunks,)),
            dma((outer,)), dma((outer,)),
            dma((inner,)), dma((inner,)),
            dma((inner,)), dma((inner,)),
            dma((outer,)), dma((outer,)),
            dma((inner,)), dma((inner,)),
            dma((inner,)), dma((inner,)),
        ],
        compiler_params=pltpu.CompilerParams(
            collective_id=0, has_side_effects=True, vmem_limit_bytes=56 * 1024 * 1024
        ),
    )(x[0], g[0], proj_in, proj_out, tests)
    return out * scale


def solution(mesh):
    return jax.shard_map(
        functools.partial(on_device, mesh.shape["ex"]),
        mesh=mesh,
        in_specs=(
            P(("grp", "ex"), None, None),
            P(("grp", "ex"), None, None),
            P(),
            P(),
            P("ex", None),
        ),
        out_specs=P(("grp", "ex"), None),
        check_vma=False,
    )
```

```python
import functools
import math

import jax
import jax.numpy as jnp
from jax import lax
from jax.experimental import pallas as pl
from jax.experimental.pallas import tpu as pltpu
from jax.sharding import PartitionSpec as P

MESH = pl.DeviceIdType.MESH
HIGHEST = lax.Precision.HIGHEST
F32 = jnp.float32
BF16 = jnp.bfloat16
DAMP = 0.1
NT = (((1,), (1,)), ((), ()))
TN = (((0,), (0,)), ((), ()))


def eye(n):
    return lax.broadcasted_iota(jnp.int32, (n, n), 0) == lax.broadcasted_iota(
        jnp.int32, (n, n), 1
    )


def split(a):
    hi = a.astype(BF16)
    lo = (a - hi.astype(F32)).astype(BF16)
    return hi, lo


def wide_dot(a, b):
    n = b.shape[1]
    row = jnp.concatenate(split(b), axis=1)
    both = jnp.dot(
        jnp.concatenate(split(a), axis=1),
        jnp.concatenate([row, row], axis=0),
        preferred_element_type=F32,
    )
    return both[:, :n] + both[:, n:]


def plan(n, target=2e-3):
    low, high = DAMP / n, 1.0 + DAMP / n
    err = (high - low) / (high + low)
    factors = []
    while err > target:
        factors.append(2.0 / (2.0 - err * err))
        err = err * err / (2.0 - err * err)
    return 2.0 / (high + low), factors


def inverses(sums):
    state = []
    for s, n in sums:
        size = s.shape[0]
        diag = eye(size)
        trace = jnp.sum(
            jnp.sum(jnp.where(diag, s, 0.0), axis=1, keepdims=True), axis=0, keepdims=True
        )
        inv_trace = 1.0 / trace
        b = s * inv_trace + jnp.where(diag, DAMP / n, 0.0)
        first, factors = plan(n)
        if size > n:
            beyond = lax.broadcasted_iota(jnp.int32, (size, size), 0) >= n
            b = jnp.where(diag & beyond, 1.0 / first, b)
        x = jnp.where(diag, first, 0.0)
        y = first * b
        state.append([b, x, y, inv_trace, factors, first])
    for step in range(max(len(st[4]) for st in state)):
        for st in state:
            b, x, y, _, factors, plan_first = st
            if step >= len(factors):
                continue
            n = b.shape[0]
            c = factors[step]
            if step == 0:
                yy = wide_dot(y, y)
                xy = plan_first * y
            else:
                prod = wide_dot(jnp.concatenate([x, y], axis=0), y)
                xy, yy = prod[:n], prod[n:]
            st[1] = c * (2.0 * x - xy)
            st[2] = c * (2.0 * y - yy)
    out = []
    for b, x, _, inv_trace, _, _ in state:
        n = b.shape[0]
        rest = jnp.where(eye(n), 1.0, 0.0) - jnp.dot(
            b, x, precision=HIGHEST, preferred_element_type=F32
        )
        out.append((x + wide_dot(x, rest)) * inv_trace)
    return out


def kernel(
    inner, outer, chunks, tokens,
    x_hbm, g_hbm, pin_hbm, pout_hbm, test_hbm, out_ref,
    x_buf, g_buf, pin_buf, pout_buf, tests, cov, moments, rs_buf, z_buf, full, grads,
    pre, flat, sbuf, rbuf, acc,
    in_sem, t_send, t_recv, rs_send, rs_recv, g_send, g_recv, z_send, z_recv,
    ag_send, ag_recv, s_send, s_recv,
):
    k_in, k_out = pin_buf.shape[0], pout_buf.shape[0]
    me = lax.axis_index("ex")
    p, z = lax.rem(me, inner), lax.div(me, inner)
    rows = moments.shape[0] // inner
    step_cols = x_buf.shape[2]

    def at_inner(k):
        return z * inner + lax.rem(p + k, inner)

    def at_outer(k):
        return lax.rem(z + k, outer) * inner + p

    def remote(src, dst, send, recv, device):
        return pltpu.make_async_remote_copy(
            src_ref=src, dst_ref=dst, send_sem=send, recv_sem=recv,
            device_id={"ex": device}, device_id_type=MESH,
        )

    barrier = pltpu.get_barrier_semaphore()
    for k in range(1, inner):
        pl.semaphore_signal(barrier, inc=1, device_id={"ex": at_inner(k)}, device_id_type=MESH)
    for k in range(1, outer):
        pl.semaphore_signal(barrier, inc=1, device_id={"ex": at_outer(k)}, device_id_type=MESH)

    pout_load = pltpu.make_async_copy(pout_hbm, pout_buf, in_sem.at[0])
    own_tests = pltpu.make_async_copy(test_hbm, tests.at[z], in_sem.at[1])

    def pin_load(i):
        cols = slice(i * step_cols, (i + 1) * step_cols)
        return pltpu.make_async_copy(
            pin_hbm.at[:, cols], pin_buf.at[:, cols], in_sem.at[4 + chunks + i]
        )

    def x_load(i):
        return pltpu.make_async_copy(
            x_hbm.at[:, i * step_cols : (i + 1) * step_cols], x_buf.at[i], in_sem.at[4 + i]
        )

    mid = g_buf.shape[0] // 2
    quarter = mid // 2
    g_loads = [
        pltpu.make_async_copy(
            g_hbm.at[pl.ds(h * mid, mid)], g_buf.at[pl.ds(h * mid, mid)], in_sem.at[2 + h]
        )
        for h in range(2)
    ]
    pout_load.start()
    for c in g_loads:
        c.start()
    for i in range(chunks):
        pin_load(i).start()
        x_load(i).start()
    own_tests.start()

    test_copies = [
        remote(test_hbm, tests.at[z], t_send.at[k], t_recv.at[k], at_outer(k))
        for k in range(1, outer)
    ]
    pout_load.wait()
    halves = (slice(0, mid), slice(mid, 2 * mid))
    backs = []
    for h in range(2):
        g_loads[h].wait()
        backs += [
            lax.dot_general(
                g_buf[q : q + quarter, :], pout_buf[...], NT, preferred_element_type=F32
            ).astype(BF16)
            for q in (h * mid, h * mid + quarter)
        ]
    pl.semaphore_wait(barrier, inner + outer - 2)
    for c in test_copies:
        c.start()
    for i in range(chunks):
        pin_load(i).wait()
        x_load(i).wait()
        weights = pin_buf[:, i * step_cols : (i + 1) * step_cols]
        feats = [
            lax.dot_general(x_buf[i, h, :], weights, NT, preferred_element_type=F32)
            for h in halves
        ]
        for h, feat in zip(halves, feats):
            if i == 0:
                acc[h, :] = feat
            elif i < chunks - 1:
                acc[h, :] += feat
    lasts = [acc[h, :] + feat for h, feat in zip(halves, feats)]
    parts = []
    for h in range(2):
        back = jnp.concatenate(backs[2 * h : 2 * h + 2], axis=0)
        both = jnp.concatenate([lasts[h].astype(BF16), back], axis=1)
        parts.append(lax.dot_general(both, both, TN, preferred_element_type=F32))
    cov[...] = parts[0] + parts[1]

    half = k_in // 2
    moments[0:half, :] = cov[0:half, 0:k_in]
    moments[half:k_in, half:k_in] = cov[half:k_in, half:k_in]
    moments[half:k_in, 0:half] = cov[k_in : k_in + k_out, k_in : k_in + k_out]
    grads[p] = cov[k_in : k_in + k_out, 0:k_in]

    rs_copies = []
    for k in range(1, inner):
        peer = lax.rem(p + k, inner)
        rs_copies.append(
            remote(
                moments.at[pl.ds(pl.multiple_of(peer * rows, 8), rows)],
                rs_buf.at[p], rs_send.at[k], rs_recv.at[k], at_inner(k),
            )
        )
    for c in rs_copies:
        c.start()
    rs_buf[p] = moments[pl.ds(pl.multiple_of(p * rows, 8), rows), :]
    for c in rs_copies:
        c.wait_recv()
    part = rs_buf[0]
    for j in range(1, inner):
        part = part + rs_buf[j]
    z_buf[z] = part
    z_copies = [
        remote(z_buf.at[z], z_buf.at[z], z_send.at[k], z_recv.at[k], at_outer(k))
        for k in range(1, outer)
    ]
    for c in z_copies:
        c.start()
    g_copies = [
        remote(grads.at[p], grads.at[p], g_send.at[k], g_recv.at[k], at_inner(k))
        for k in range(1, inner)
    ]
    for c in g_copies:
        c.start()
    for c in z_copies:
        c.wait_recv()
    total = z_buf[0]
    for j in range(1, outer):
        total = total + z_buf[j]
    mine = full.at[pl.ds(pl.multiple_of(p * rows, 8), rows)]
    mine[...] = total
    ag_copies = [
        remote(mine, mine, ag_send.at[k], ag_recv.at[k], at_inner(k)) for k in range(1, inner)
    ]
    for c in ag_copies:
        c.start()
    for c in ag_copies:
        c.wait_recv()

    top, low = full[0:half, :], full[half:k_in, :]
    corner = jnp.concatenate([top.T[half:k_in, :], low[:, half:]], axis=1)
    sum_in = jnp.concatenate([top, corner], axis=0)
    sum_out = jnp.concatenate([low[:, 0:half], jnp.zeros((half, half), F32)], axis=1)
    sum_out = jnp.concatenate([sum_out, jnp.zeros((half, k_in), F32)], axis=0)
    inv_in, inv_out = inverses([(sum_in, k_in), (sum_out, k_out)])
    inv_in = inv_in * tokens
    inv_out = inv_out[0:k_out, 0:k_out] * tokens
    for c in g_copies:
        c.wait_recv()
    batch = max(inner // 2, 1)
    rights = [
        jnp.dot(
            grads[e : e + batch].reshape(batch * k_out, k_in), inv_in,
            precision=HIGHEST, preferred_element_type=F32,
        )
        for e in range(0, inner, batch)
    ]
    for e in range(batch):
        for r, right in enumerate(rights):
            at = (r * batch + e) * k_out
            pre[at : at + k_out, :] = jnp.dot(
                inv_out, right[e * k_out : (e + 1) * k_out],
                precision=HIGHEST, preferred_element_type=F32,
            )
    for o in range(k_out):
        flat[:, o * k_in : (o + 1) * k_in] = pre[pl.ds(o, inner, stride=k_out), :]
    precond = flat[...].astype(BF16)

    own_tests.wait()
    for c in test_copies:
        c.wait_recv()
    per = tests.shape[1]
    width = out_ref.shape[1]
    block = lax.dot_general(
        precond, jnp.concatenate([tests[j] for j in range(outer)], axis=0), NT,
        preferred_element_type=F32,
    )
    held = lax.broadcasted_iota(jnp.int32, (outer * per, width), 0)
    place = (lax.div(held, per) * inner + p) * per + lax.rem(held, per)
    put = lax.broadcasted_iota(jnp.int32, (outer * per, width), 1) == place
    placed = jnp.dot(
        block, jnp.where(put, 1.0, 0.0), precision=HIGHEST, preferred_element_type=F32
    )
    for e in range(inner):
        sbuf[e] = placed[e : e + 1]
    s_copies = [
        remote(
            sbuf.at[lax.rem(p + k, inner)], rbuf.at[p], s_send.at[k], s_recv.at[k], at_inner(k)
        )
        for k in range(1, inner)
    ]
    for c in s_copies:
        c.start()
    rbuf[p] = sbuf[p]
    for c in s_copies:
        c.wait_recv()
    score = rbuf[0]
    for j in range(1, inner):
        score = score + rbuf[j]
    out_ref[...] = score
    for group in (test_copies, rs_copies, z_copies, g_copies, ag_copies, s_copies):
        for c in group:
            c.wait_send()


def on_device(devices, x, g, proj_in, proj_out, tests):
    _, tok, _ = x.shape
    k_in, k_out = proj_in.shape[0], proj_out.shape[0]
    inner = math.gcd(devices, 8)
    outer = devices // inner
    per = tests.shape[0]
    chunks = 8
    total_tokens = tok * devices
    scale = 4.0 / (k_in * k_out * tok) ** 0.5
    height = k_in + k_out
    any_space = pl.BlockSpec(memory_space=pl.ANY)
    dma = pltpu.SemaphoreType.DMA
    out = pl.pallas_call(
        functools.partial(kernel, inner, outer, chunks, float(total_tokens)),
        out_shape=jax.ShapeDtypeStruct((1, per * devices), F32),
        in_specs=[any_space] * 5,
        out_specs=pl.BlockSpec(memory_space=pltpu.VMEM),
        scratch_shapes=[
            pltpu.VMEM((chunks, tok, x.shape[2] // chunks), BF16),
            pltpu.VMEM(g.shape[1:], BF16),
            pltpu.VMEM(proj_in.shape, BF16),
            pltpu.VMEM(proj_out.shape, BF16),
            pltpu.VMEM((outer,) + tests.shape, BF16),
            pltpu.VMEM((height, height), F32),
            pltpu.VMEM((k_in, k_in), F32),
            pltpu.VMEM((inner, k_in // inner, k_in), F32),
            pltpu.VMEM((outer, k_in // inner, k_in), F32),
            pltpu.VMEM((k_in, k_in), F32),
            pltpu.VMEM((inner, k_out, k_in), F32),
            pltpu.VMEM((inner * k_out, k_in), F32),
            pltpu.VMEM((inner, k_out * k_in), F32),
            pltpu.VMEM((inner, 1, per * devices), F32),
            pltpu.VMEM((inner, 1, per * devices), F32),
            pltpu.VMEM((tok, k_in), F32),
            dma((4 + 2 * chunks,)),
            dma((outer,)), dma((outer,)),
            dma((inner,)), dma((inner,)),
            dma((inner,)), dma((inner,)),
            dma((outer,)), dma((outer,)),
            dma((inner,)), dma((inner,)),
            dma((inner,)), dma((inner,)),
        ],
        compiler_params=pltpu.CompilerParams(
            collective_id=0, has_side_effects=True, vmem_limit_bytes=56 * 1024 * 1024
        ),
    )(x[0], g[0], proj_in, proj_out, tests)
    return out * scale


def solution(mesh):
    return jax.shard_map(
        functools.partial(on_device, mesh.shape["ex"]),
        mesh=mesh,
        in_specs=(
            P(("grp", "ex"), None, None),
            P(("grp", "ex"), None, None),
            P(),
            P(),
            P("ex", None),
        ),
        out_specs=P(("grp", "ex"), None),
        check_vma=False,
    )
```
